256 devices in a mesh: band: 4 (over x), dom: 64 (over y, z, core).
Axes of the slice: x: 4, y: 4, z: 8, core: 2. Of those that a mesh axis runs over, the one named last changes fastest.
Arguments:
- orbitals: float32 [128, 32, 32, 1024], P('dom', None, None, 'band'), may hold values from -6 to 6
- potential: float32 [128, 32, 32], P('dom'), may hold values from -2 to 2
- projectors: float32 [8192, 8, 256], P('dom'), may hold values from -0.375 to 0.375
- tile_cells: int32 [8192, 256], P('dom'), may hold values from 0 to 2047
- tile_atom: int32 [8192], replicated, may hold values from -1 to 511, as said below
- atom_owner: int32 [512], replicated, may hold values from 0 to 511, as said below
- coupling: float32 [512, 8, 8], P('dom'), may hold values from -2 to 2
- rotation: float32 [1024, 1024], P(None, 'band'), may hold values from -0.1875 to 0.1875
Outputs:
- rotated_orbitals: float32 [128, 32, 32, 1024], P('dom', None, None, 'band')
- rotated_applied: float32 [128, 32, 32, 1024], P('dom', None, None, 'band')
The draws below stay inside these ranges and needn't reach their ends.
Inputs may be any that keep to these rules, and one draw needn't show every extreme that they name: `tile_atom`: tile slots come in blocks of 128, one block a domain; in each block the used slots come first, at least half of them are used, and some block is full. An atom a is owned by domain atom_owner[a] // 8. The tiles of one domain name atoms of any one owning domain at most 4 times, and some owning domain is named exactly 4 times by every domain. `atom_owner`: each row of the coupling table belongs to exactly one atom.
All inputs are finite; a program needn't handle non-finite values.
Results may differ from the reference program's by a relative error of at most 0.000071.
Values sent between devices are 32-bit elements; how exact they have to be, the bound alone decides.
No kernel may reach another device: no remote copies, remote signals or barrier semaphores. Data moves between devices by JAX's collectives and lax.ppermute only.
A program may use at most 128 MiB of HBM per device.

```python
import jax
import jax.numpy as jnp
from jax import lax

BANDS = 1024
NPROJ = 8
CX = 2
NY = 32
NZ = 32
TILE = 256
E_DEV = 128
ATOM_DEV = 8
NX = 128
NATOM = 512
ENTRIES = 8192
N_DOM = 64


def domain_order(pool_key):
    return jax.random.permutation(pool_key, N_DOM * max(2, 2 * E_DEV // N_DOM))


def atom_tables(key):
    atom_total = ATOM_DEV * N_DOM
    capacity = max(2, 2 * E_DEV // N_DOM)
    pool_size = N_DOM * capacity
    atom_rows = jax.random.permutation(jax.random.fold_in(key, 11), atom_total).astype(jnp.int32)
    row_atoms = jnp.argsort(atom_rows).astype(jnp.int32)
    busiest = jax.random.randint(jax.random.fold_in(key, 12), (), 0, N_DOM)
    fullest = jax.random.randint(jax.random.fold_in(key, 13), (), 0, N_DOM)
    counts = jax.random.randint(jax.random.fold_in(key, 14), (N_DOM,), E_DEV // 2, E_DEV + 1)
    counts = jnp.where(jnp.arange(N_DOM) == fullest, E_DEV, counts)
    owner_pool = jnp.arange(pool_size, dtype=jnp.int32) // capacity
    domain_keys = jax.random.split(jax.random.fold_in(key, 15), N_DOM)
    scores = jax.vmap(domain_order)(domain_keys).astype(jnp.int32)
    scores = jnp.where(owner_pool[None, :] == busiest, scores - pool_size, scores)
    picked = jnp.argsort(scores, axis=1)[:, :E_DEV]
    owners = owner_pool[picked]
    slot_draw = jax.random.randint(jax.random.fold_in(key, 16), (N_DOM, E_DEV), 0, ATOM_DEV)
    atom_ids = row_atoms[owners * ATOM_DEV + slot_draw]
    used_mask = jnp.arange(E_DEV)[None, :] < counts[:, None]
    tile_list = jnp.where(used_mask, atom_ids, -1).reshape(-1).astype(jnp.int32)
    return (atom_rows, tile_list)


def draw_tile_atom(key, part):
    return atom_tables(key)[1]


def draw_atom_owner(key, part):
    return atom_tables(key)[0]


def touch_ends(array, key, low, high):
    dims = array.shape
    spot = [jax.random.randint(jax.random.fold_in(key, axis), (), 0, dims[axis]) for axis in range(len(dims))]
    array = array.at[tuple(spot)].set(low)
    longest = dims.index(max(dims))
    spot[longest] = (spot[longest] + 1) % dims[longest]
    return array.at[tuple(spot)].set(high)


def block_scale(rng, shape, cuts, smallest, top_value):
    factor_of = 1.0
    for axis_at, blocks in cuts:
        draws = jax.random.uniform(jax.random.fold_in(jax.random.fold_in(rng, 6), axis_at), (blocks,), jnp.float32, smallest / len(cuts), top_value / len(cuts))
        factor_of = factor_of * jnp.repeat(jnp.exp(draws), shape[axis_at] // blocks).reshape((-1,) + (1,) * (len(shape) - 1 - axis_at))
    return factor_of


def normal_values(key, shape, scale, bound, shards=(), kind=jnp.bfloat16):
    values = jax.random.normal(key, shape, jnp.float32) * scale
    if len(shards) > 0:
        values = block_scale(key, shape, shards, -0.22, 0.18) * values
    return jnp.clip(values, min=-bound, max=bound).astype(kind)


def setup_inputs(seed: int = 0) -> dict:
    key_list = jax.random.split(jax.random.key(seed), 9)
    return {
        "orbitals": normal_values(key_list[0], (NX, NY, NZ, BANDS), 1.0, 6.0, ((0, 64), (3, 4)), jnp.float32),
        "potential": jnp.clip(jax.random.uniform(key_list[1], (NX, NY, NZ), jnp.float32, -2.0, 2.0) * block_scale(key_list[1], (NX, NY, NZ), ((0, 64),), -0.4, 0.0), -2.0, 2.0),
        "projectors": normal_values(key_list[2], (ENTRIES, NPROJ, TILE), TILE ** -0.5, 0.375, ((0, 64),), jnp.float32),
        "tile_cells": touch_ends(jax.random.randint(key_list[3], (ENTRIES, TILE), 0, CX * NY * NZ), jax.random.fold_in(key_list[3], 1), 0, (CX * NY * NZ) - 1).astype(jnp.int32),
        "tile_atom": draw_tile_atom(jax.random.fold_in(key_list[8], 71), 0),
        "atom_owner": draw_atom_owner(jax.random.fold_in(key_list[8], 71), 0),
        "coupling": normal_values(key_list[6], (NATOM, NPROJ, NPROJ), NPROJ ** -0.5, 2.0, ((0, 64),), jnp.float32),
        "rotation": normal_values(key_list[7], (BANDS, BANDS), BANDS ** -0.5, 0.1875, ((1, 4),), jnp.float32),
    }


def neighbor_sum(field):
    summed = jnp.roll(field, 1, 0) + jnp.roll(field, -1, 0)
    summed = summed + jnp.roll(field, 1, 1) + jnp.roll(field, -1, 1)
    return summed + jnp.roll(field, 1, 2) + jnp.roll(field, -1, 2)


def reference(orbitals, potential, projectors, tile_cells, tile_atom, atom_owner, coupling, rotation):
    band_count = orbitals.shape[3]
    cell_count = CX * NY * NZ
    applied_local = (3.0 + potential[..., None]) * orbitals - 0.5 * neighbor_sum(orbitals)
    domain_fields = orbitals.reshape(N_DOM, cell_count, band_count)
    domain_cells = tile_cells.reshape(N_DOM, E_DEV, TILE)
    domain_projectors = projectors.reshape(N_DOM, E_DEV, NPROJ, TILE)

    def project(inputs):
        domain_field, tile_index, values = inputs
        gathered = jnp.take(domain_field, tile_index.reshape(-1), axis=0).reshape(E_DEV, TILE, band_count)
        return jnp.einsum("ekt,etb->ekb", values, gathered, precision=lax.Precision.HIGHEST)

    partials = lax.map(project, (domain_fields, domain_cells, domain_projectors)).reshape(ENTRIES, NPROJ, band_count)
    used_mask = tile_atom >= 0
    segment = jnp.where(used_mask, tile_atom, NATOM).astype(jnp.int32)
    atom_sums = jax.ops.segment_sum(partials, segment, num_segments=NATOM + 1)[:NATOM]
    atom_coupling = coupling[atom_owner]
    scaled = jnp.einsum("akj,ajb->akb", atom_coupling, atom_sums, precision=lax.Precision.HIGHEST)
    safe_atom = jnp.where(used_mask, tile_atom, 0).astype(jnp.int32)
    returned = jnp.take(scaled, safe_atom, axis=0) * used_mask[:, None, None].astype(jnp.float32)
    domain_returned = returned.reshape(N_DOM, E_DEV, NPROJ, band_count)

    def expand(inputs):
        tile_index, values, coefficient = inputs
        spread = jnp.einsum("ekt,ekb->etb", values, coefficient, precision=lax.Precision.HIGHEST)
        spread = spread.reshape(E_DEV * TILE, band_count)
        return jnp.zeros((cell_count, band_count), jnp.float32).at[tile_index.reshape(-1)].add(spread)

    applied_far = lax.map(expand, (domain_cells, domain_projectors, domain_returned)).reshape(orbitals.shape)
    applied = applied_local + applied_far
    rotated_orbitals = jnp.dot(orbitals.reshape(-1, band_count), rotation, precision=lax.Precision.HIGHEST, preferred_element_type=jnp.float32).reshape(orbitals.shape)
    rotated_applied = jnp.dot(applied.reshape(-1, band_count), rotation, precision=lax.Precision.HIGHEST, preferred_element_type=jnp.float32).reshape(orbitals.shape)
    return rotated_orbitals, rotated_applied
```

```python
import functools

import jax
import jax.numpy as jnp
from jax import lax
from jax.experimental import pallas as pl
from jax.experimental.pallas import tpu as pltpu
from jax.sharding import PartitionSpec as P


F32, BF16 = jnp.float32, jnp.bfloat16
Y, Z, C = 4, 8, 2
OWN = 8
NP = 8
TILES = 128
TILE = 256
CELLS = 2048
PLANE = 1024
W = 256
STEP_TILES = 32
GROUP = 8
HI, LO = 8, 256
SLOTS = Y * Z * OWN
ALL = C * SLOTS
VMEM = 56 << 20


def split(x):
    hi = x.astype(BF16)
    return hi, (x - hi.astype(F32)).astype(BF16)


def dot3(a_hi, a_lo, b_hi, b_lo, dims):
    dot = functools.partial(
        lax.dot_general, dimension_numbers=(dims, ((), ())), preferred_element_type=F32
    )
    return dot(a_hi, b_hi) + (dot(a_lo, b_hi) + dot(a_hi, b_lo))


def slot_of(atom, owner_ref):
    me = lax.axis_index("dom")
    row = owner_ref[jnp.maximum(atom, 0)]
    owner = row // OWN
    core = jnp.bitwise_xor(owner, me) & 1
    y = (owner // (Z * C) - me // (Z * C)) & (Y - 1)
    z = (owner // C) & (Z - 1)
    slot = ((core * Y + y) * Z + z) * OWN + (row & (OWN - 1))
    return jnp.where(atom >= 0, slot, ALL)


def project_kernel(
    owner_ref, atom_ref, proj_ref, cell_ref, x_ref,
    keep_ref, send_ref, dhi_ref, dlo_ref, slot_ref,
    xhi_ref, xlo_ref, dense_ref, part_ref, sums_ref, mine_ref, sem,
):
    step = pl.program_id(0)

    @pl.when(step == 0)
    def _():
        first = pl.multiple_of(lax.axis_index("dom") * TILES, TILES)
        copy = pltpu.make_async_copy(atom_ref.at[pl.ds(first, TILES)], mine_ref, sem)
        copy.start()
        sums_ref[...] = jnp.zeros_like(sums_ref)
        hi, lo = split(x_ref[...])
        xhi_ref[...] = hi
        xlo_ref[...] = lo
        copy.wait()

    lo_ids = lax.broadcasted_iota(jnp.int32, (LO, TILE), 0).astype(F32).astype(BF16)
    pair_ids = (lax.broadcasted_iota(jnp.int32, (2 * NP, TILE), 0) // NP).astype(F32)
    one, zero = jnp.ones((), BF16), jnp.zeros((), BF16)

    def densify(group, carry):
        for i in range(GROUP):
            e = group * GROUP + i
            slot_ref[step * STEP_TILES + e] = slot_of(
                mine_ref[step * STEP_TILES + e], owner_ref
            )
            cells = cell_ref[pl.ds(e, 1), :]
            v_hi, v_lo = split(proj_ref[e])
            v_hi = jnp.concatenate([v_hi, v_hi], axis=0)
            v_lo = jnp.concatenate([v_lo, v_lo], axis=0)
            high = jnp.broadcast_to((cells // LO).astype(F32), (2 * NP, TILE)) - pair_ids
            high = high.astype(BF16)
            hits = [high == jnp.full((), 2.0 * h, BF16) for h in range(HI // 2)]
            spread = jnp.concatenate(
                [jnp.where(hit, v, zero) for v in (v_hi, v_lo) for hit in hits], axis=0
            )
            low = (cells & (LO - 1)).astype(F32).astype(BF16)
            hot = jnp.where(jnp.broadcast_to(low, (LO, TILE)) == lo_ids, one, zero)
            both = lax.dot_general(
                spread, hot, (((1,), (1,)), ((), ())), preferred_element_type=F32
            )
            sums = both[: HI * NP] + both[HI * NP :]
            rows = pl.ds(pl.multiple_of(e * NP, NP), NP)
            for h in range(HI):
                dense_ref[rows, h * LO : (h + 1) * LO] = sums[h * NP : (h + 1) * NP]
        return carry

    lax.fori_loop(0, STEP_TILES // GROUP, densify, 0)
    d_hi, d_lo = split(dense_ref[...])
    dhi_ref[...] = d_hi
    dlo_ref[...] = d_lo
    rows = STEP_TILES * NP
    dot = functools.partial(
        lax.dot_general, dimension_numbers=(((1,), (0,)), ((), ())), preferred_element_type=F32
    )
    upper = dot(jnp.concatenate([d_hi, d_lo], axis=0), xhi_ref[...])
    part_ref[...] = upper[:rows] + (upper[rows:] + dot(d_hi, xlo_ref[...]))

    def add(e, carry):
        slot = slot_ref[step * STEP_TILES + e]
        value = part_ref[pl.ds(pl.multiple_of(e * NP, NP), NP), :]
        sums_ref[slot] = sums_ref[slot] + value
        return carry

    lax.fori_loop(0, STEP_TILES, add, 0, unroll=8)

    @pl.when(step == TILES // STEP_TILES - 1)
    def _():
        keep_ref[...] = sums_ref[:SLOTS]
        send_ref[...] = sums_ref[SLOTS:ALL]


def project(tile_atom, atom_owner, projectors, tile_cells, x):
    rows = STEP_TILES * NP
    return pl.pallas_call(
        project_kernel,
        out_shape=(
            jax.ShapeDtypeStruct((SLOTS, NP, W), F32),
            jax.ShapeDtypeStruct((SLOTS, NP, W), F32),
            pltpu.HBM((TILES * NP, CELLS), BF16),
            pltpu.HBM((TILES * NP, CELLS), BF16),
            jax.ShapeDtypeStruct((TILES,), jnp.int32),
        ),
        grid_spec=pltpu.PrefetchScalarGridSpec(
            num_scalar_prefetch=1,
            grid=(TILES // STEP_TILES,),
            in_specs=[
                pl.BlockSpec(memory_space=pl.ANY),
                pl.BlockSpec((STEP_TILES, NP, TILE), lambda i, *_: (i, 0, 0)),
                pl.BlockSpec((STEP_TILES, TILE), lambda i, *_: (i, 0)),
                pl.BlockSpec((CELLS, W), lambda i, *_: (0, 0)),
            ],
            out_specs=[
                pl.BlockSpec((SLOTS, NP, W), lambda i, *_: (0, 0, 0)),
                pl.BlockSpec((SLOTS, NP, W), lambda i, *_: (0, 0, 0)),
                pl.BlockSpec((rows, CELLS), lambda i, *_: (i, 0)),
                pl.BlockSpec((rows, CELLS), lambda i, *_: (i, 0)),
                pl.BlockSpec(memory_space=pltpu.SMEM),
            ],
            scratch_shapes=[
                pltpu.VMEM((CELLS, W), BF16),
                pltpu.VMEM((CELLS, W), BF16),
                pltpu.VMEM((rows, CELLS), F32),
                pltpu.VMEM((rows, W), F32),
                pltpu.VMEM((ALL + 1, NP, W), F32),
                pltpu.SMEM((TILES,), jnp.int32),
                pltpu.SemaphoreType.DMA(()),
            ],
        ),
        compiler_params=pltpu.CompilerParams(vmem_limit_bytes=VMEM),
        name="project",
    )(atom_owner, tile_atom, projectors, tile_cells, x)


def couple_kernel(coupling_ref, sums_ref, out_ref):
    sums = sums_ref[0]
    for z in range(1, Z):
        sums = sums + sums_ref[z]
    for r in range(OWN):
        matrix = coupling_ref[r]
        total = matrix[:, 0:1] * sums[r, 0:1, :]
        for j in range(1, NP):
            total = total + matrix[:, j : j + 1] * sums[r, j : j + 1, :]
        out_ref[r * NP : (r + 1) * NP, :] = total


def couple(coupling, sums):
    return pl.pallas_call(
        couple_kernel, out_shape=jax.ShapeDtypeStruct((OWN * NP, W), F32), name="couple"
    )(coupling, sums)


def relative_rows(rotation_ref, offset):
    band = (lax.axis_index("band") + offset) & 3
    return rotation_ref[pl.ds(pl.multiple_of(band * W, W), W), :]


def turn_small_kernel(rotation_ref, mine_ref, right_ref, far_ref, left_ref, out_ref):
    total = None
    for offset, ref in enumerate((mine_ref, right_ref, far_ref, left_ref)):
        term = dot3(*split(ref[...]), *split(relative_rows(rotation_ref, offset)), ((1,), (0,)))
        total = term if total is None else total + term
    for z in range(Z):
        out_ref[z] = total


def turn_small(rotation, *pieces):
    return pl.pallas_call(
        turn_small_kernel, out_shape=jax.ShapeDtypeStruct((Z, OWN * NP, W), F32), name="turn_small"
    )(rotation, *pieces)


ROWS = 256


def turn_kernel(
    rotation_ref, mine_ref, right_a_ref, right_b_ref, left_a_ref, left_b_ref, far_a_ref,
    far_b_ref, out_ref, first_ref, second_ref, rhi_ref, rlo_ref, xhi_ref, xlo_ref,
):
    step = pl.program_id(0)
    low = step < PLANE // ROWS

    @pl.when(step == 0)
    def _():
        for offset in range(4):
            hi, lo = split(relative_rows(rotation_ref, offset))
            rhi_ref[offset * W : (offset + 1) * W, :] = hi
            rlo_ref[offset * W : (offset + 1) * W, :] = lo

    def of_plane(a_ref, b_ref):
        return jnp.where(low, a_ref[...], b_ref[...])

    values = (
        mine_ref[...],
        of_plane(right_a_ref, right_b_ref),
        of_plane(far_a_ref, far_b_ref),
        of_plane(left_a_ref, left_b_ref),
    )
    for offset, value in enumerate(values):
        hi, lo = split(value)
        xhi_ref[:, offset * W : (offset + 1) * W] = hi
        xlo_ref[:, offset * W : (offset + 1) * W] = lo
    result = dot3(xhi_ref[...], xlo_ref[...], rhi_ref[...], rlo_ref[...], ((1,), (0,)))
    out_ref[...] = result

    @pl.when(low)
    def _():
        first_ref[...] = result

    @pl.when(jnp.logical_not(low))
    def _():
        second_ref[...] = result


def turn(rotation, mine, right_a, right_b, left_a, left_b, far_a, far_b):
    half = PLANE // ROWS
    block = pl.BlockSpec((ROWS, W), lambda i: (i, 0))
    first = pl.BlockSpec((ROWS, W), lambda i: (jnp.minimum(i, half - 1), 0))
    second = pl.BlockSpec((ROWS, W), lambda i: (jnp.maximum(i - half, 0), 0))
    return pl.pallas_call(
        turn_kernel,
        out_shape=(
            jax.ShapeDtypeStruct((CELLS, W), F32),
            jax.ShapeDtypeStruct((PLANE, W), F32),
            jax.ShapeDtypeStruct((PLANE, W), F32),
        ),
        grid_spec=pl.GridSpec(
            grid=(CELLS // ROWS,),
            in_specs=[
                pl.BlockSpec((4 * W, W), lambda i: (0, 0)),
                block,
                first,
                second,
                first,
                second,
                first,
                second,
            ],
            out_specs=[block, first, second],
            scratch_shapes=[
                pltpu.VMEM((4 * W, W), BF16),
                pltpu.VMEM((4 * W, W), BF16),
                pltpu.VMEM((ROWS, 4 * W), BF16),
                pltpu.VMEM((ROWS, 4 * W), BF16),
            ],
        ),
        name="turn",
    )(rotation, mine, right_a, right_b, left_a, left_b, far_a, far_b)


def stencil_kernel(potential_ref, mine_ref, other_ref, out_ref):
    side = 32

    def line(y, carry):
        here = pl.ds(pl.multiple_of(y * side, side), side)
        above = pl.ds(pl.multiple_of(((y + side - 1) & (side - 1)) * side, side), side)
        below = pl.ds(pl.multiple_of(((y + 1) & (side - 1)) * side, side), side)
        value = mine_ref[here, :]
        beside = other_ref[here, :] + (mine_ref[above, :] + mine_ref[below, :])
        beside = beside + (pltpu.roll(value, 1, 0) + pltpu.roll(value, side - 1, 0))
        out_ref[here, :] = (3.0 + potential_ref[here, :]) * value - 0.5 * beside
        return carry

    lax.fori_loop(0, side, line, 0, unroll=4)


def stencil(potential, value):
    return pl.pallas_call(
        stencil_kernel,
        out_shape=jax.ShapeDtypeStruct((CELLS, W), F32),
        grid_spec=pl.GridSpec(
            grid=(2,),
            in_specs=[
                pl.BlockSpec((PLANE, 1), lambda i: (i, 0)),
                pl.BlockSpec((PLANE, W), lambda i: (i, 0)),
                pl.BlockSpec((PLANE, W), lambda i: (1 - i, 0)),
            ],
            out_specs=pl.BlockSpec((PLANE, W), lambda i: (i, 0)),
        ),
        name="stencil",
    )(potential, value, value)


PIECES = (64, 64, 32, 32, 64)


def expand_kernel(*refs):
    slot_ref, pieces = refs[0], refs[1:11]
    dhi_ref, dlo_ref, local_ref, before_ref, after_ref = refs[11:16]
    out_ref, all_ref, back_ref, bhi_ref, blo_ref, sems = refs[16:]
    step = pl.program_id(0)

    @pl.when(step == 0)
    def _():
        copies, start = [], 0
        for i, piece in enumerate(pieces):
            size = PIECES[i % len(PIECES)]
            copies.append(
                pltpu.make_async_copy(piece, all_ref.at[pl.ds(start, size)], sems.at[i])
            )
            start += size
        for copy in copies:
            copy.start()
        all_ref[ALL] = jnp.zeros((NP, W), F32)
        for copy in copies:
            copy.wait()

        def take(e, carry):
            back_ref[pl.ds(pl.multiple_of(e * NP, NP), NP), :] = all_ref[slot_ref[e]]
            return carry

        lax.fori_loop(0, TILES, take, 0, unroll=16)
        hi, lo = split(back_ref[...].T)
        bhi_ref[...] = hi
        blo_ref[...] = lo

    halo = jnp.where(step < PLANE // ROWS, before_ref[...], after_ref[...])
    far = dot3(bhi_ref[...], blo_ref[...], dhi_ref[...], dlo_ref[...], ((1,), (0,)))
    out_ref[...] = (local_ref[...] - 0.5 * halo) + far.T


def expand(slots, pieces, d_hi, d_lo, local, before, after):
    d_hi, d_lo, local = (
        pltpu.with_memory_space_constraint(v, pltpu.HBM) for v in (d_hi, d_lo, local)
    )
    half = PLANE // ROWS
    dense = pl.BlockSpec((TILES * NP, ROWS), lambda i, *_: (0, i))
    return pl.pallas_call(
        expand_kernel,
        out_shape=jax.ShapeDtypeStruct((CELLS, W), F32),
        grid_spec=pltpu.PrefetchScalarGridSpec(
            num_scalar_prefetch=1,
            grid=(CELLS // ROWS,),
            in_specs=[
                *[pl.BlockSpec(memory_space=pl.ANY)] * len(pieces),
                dense,
                dense,
                pl.BlockSpec((ROWS, W), lambda i, *_: (i, 0)),
                pl.BlockSpec((ROWS, W), lambda i, *_: (jnp.minimum(i, half - 1), 0)),
                pl.BlockSpec((ROWS, W), lambda i, *_: (jnp.maximum(i - half, 0), 0)),
            ],
            out_specs=pl.BlockSpec((ROWS, W), lambda i, *_: (i, 0)),
            scratch_shapes=[
                pltpu.VMEM((ALL + 1, NP, W), F32),
                pltpu.VMEM((TILES * NP, W), F32),
                pltpu.VMEM((W, TILES * NP), BF16),
                pltpu.VMEM((W, TILES * NP), BF16),
                pltpu.SemaphoreType.DMA((len(pieces),)),
            ],
        ),
        compiler_params=pltpu.CompilerParams(vmem_limit_bytes=20 << 20),
        name="expand",
    )(slots, *pieces, d_hi, d_lo, local, before, after)


def at(y, z, c):
    return (y % Y) * Z * C + (z % Z) * C + c


DEVICES = [(y, z, c) for y in range(Y) for z in range(Z) for c in range(C)]


def to_y(value, shift):
    return lax.ppermute(value, "dom", [(at(y, z, c), at(y + shift, z, c)) for y, z, c in DEVICES])


def to_core(value):
    return lax.ppermute(value, "dom", [(at(y, z, c), at(y, z, 1 - c)) for y, z, c in DEVICES])


def to_dom(value, shift):
    count = Y * Z * C
    return lax.ppermute(value, "dom", [(i, (i + shift) % count) for i in range(count)])


def to_band(value, shift):
    return lax.ppermute(value, "band", [(i, (i + shift) % 4) for i in range(4)])


Z_LINES = [[at(y, z, c) for z in range(Z)] for y in range(Y) for c in range(C)]


def swap_z(value):
    return lax.all_to_all(
        value, "dom", split_axis=0, concat_axis=0, axis_index_groups=Z_LINES, tiled=True
    )


def step(orbitals, potential, projectors, tile_cells, tile_atom, atom_owner, coupling, rotation):
    x = orbitals.reshape(CELLS, W)

    left_a = to_band(x[:PLANE], 1)
    right_b = to_band(x[PLANE:], -1)
    left_b = to_band(x[PLANE:], 1)
    right_a = to_band(x[:PLANE], -1)
    far_a = to_band(left_a, 1)
    far_b = to_band(right_b, -1)

    keep, send, d_hi, d_lo, slots = project(
        tile_atom, atom_owner, projectors, tile_cells, x
    )
    send = to_core(send)
    sums = (keep + send).reshape(Y, Z, OWN, NP, W)
    cut = Z // 2
    up = to_y(sums[2, :cut], 1)
    down = to_y(sums[2, cut:], -1)
    up_raw = to_y(sums[1, cut:], 1)
    down_raw = to_y(sums[3, :cut], -1)
    up = to_y(sums[1, :cut] + up, 1)
    down = to_y(sums[3, cut:] + down, -1)
    line = sums[0] + jnp.concatenate([up + down_raw, up_raw + down], axis=0)
    line = swap_z(line)
    scaled = couple(coupling, line)

    parts = to_band(scaled, -1), to_band(scaled, 2), to_band(scaled, 1)
    back = turn_small(rotation, scaled, *parts)

    line = swap_z(back).reshape(Z * OWN, NP, W)
    mid = Z * OWN // 2
    below_line = to_y(line, 1)
    above_line = to_y(line, -1)
    across_a = to_y(below_line[:mid], 1)
    across_b = to_y(above_line[mid:], -1)
    near = [line, above_line, across_a, across_b, below_line]
    pieces = near + [to_core(v) for v in near]

    turned, first, second = turn(
        rotation, x, right_a, right_b, left_a, left_b, far_a, far_b
    )
    before = to_dom(second, 1)
    after = to_dom(first, -1)
    local = stencil(potential.reshape(CELLS, 1), turned)
    applied = expand(slots, pieces, d_hi, d_lo, local, before, after)
    return turned.reshape(orbitals.shape), applied.reshape(orbitals.shape)


def solution(mesh):
    return jax.shard_map(
        step,
        mesh=mesh,
        in_specs=(
            P("dom", None, None, "band"),
            P("dom", None, None),
            P("dom", None, None),
            P("dom", None),
            P(),
            P(),
            P("dom", None, None),
            P(None, "band"),
        ),
        out_specs=(P("dom", None, None, "band"), P("dom", None, None, "band")),
        check_vma=False,
    )
```

```python
import functools

import jax
import jax.numpy as jnp
from jax import lax
from jax.experimental import pallas as pl
from jax.experimental.pallas import tpu as pltpu
from jax.sharding import PartitionSpec as P


F32, BF16 = jnp.float32, jnp.bfloat16
Y, Z, C = 4, 8, 2
OWN = 8
NP = 8
TILES = 128
TILE = 256
CELLS = 2048
PLANE = 1024
W = 256
STEP_TILES = 32
GROUP = 32
HI, LO = 8, 256
SLOTS = Y * Z * OWN
ALL = C * SLOTS
VMEM = 32 << 20
SMALL = pltpu.CompilerParams(vmem_limit_bytes=8 << 20)
MEDIUM = pltpu.CompilerParams(vmem_limit_bytes=20 << 20)


def in_hbm(x):
    return pltpu.with_memory_space_constraint(x, pltpu.HBM)


def outer_plane():
    return lax.axis_index("dom") & 1


def cut_kernel(x_ref, outer_ref, inner_ref, sems):
    outer = outer_plane()
    copies = [
        pltpu.make_async_copy(
            x_ref.at[pl.ds(pl.multiple_of(plane * PLANE, PLANE), PLANE)], ref, sems.at[i]
        )
        for i, (plane, ref) in enumerate(((outer, outer_ref), (1 - outer, inner_ref)))
    ]
    for copy in copies:
        copy.start()
    for copy in copies:
        copy.wait()


def cut_planes(x):
    plane = jax.ShapeDtypeStruct((PLANE, W), F32)
    return pl.pallas_call(
        cut_kernel,
        out_shape=(plane, plane),
        in_specs=[pl.BlockSpec(memory_space=pl.ANY)],
        out_specs=[pl.BlockSpec(memory_space=pltpu.VMEM)] * 2,
        scratch_shapes=[pltpu.SemaphoreType.DMA((2,))],
        compiler_params=SMALL,
        name="cut",
    )(in_hbm(x))


def split(x):
    hi = x.astype(BF16)
    return hi, (x - hi.astype(F32)).astype(BF16)


def dot3(a_hi, a_lo, b_hi, b_lo, dims):
    dot = functools.partial(
        lax.dot_general, dimension_numbers=(dims, ((), ())), preferred_element_type=F32
    )
    return dot(a_hi, b_hi) + (dot(a_lo, b_hi) + dot(a_hi, b_lo))


def slot_of(atom, owner_ref):
    me = lax.axis_index("dom")
    row = owner_ref[jnp.maximum(atom, 0)]
    owner = row // OWN
    core = jnp.bitwise_xor(owner, me) & 1
    y = (owner // (Z * C) - me // (Z * C)) & (Y - 1)
    z = (owner // C) & (Z - 1)
    slot = ((core * Y + y) * Z + z) * OWN + (row & (OWN - 1))
    return jnp.where(atom >= 0, slot, ALL)


def project_kernel(
    owner_ref, atom_ref, proj_ref, cell_ref, x_ref,
    keep_ref, send_ref, dhi_ref, dlo_ref, slot_ref,
    xhi_ref, xlo_ref, dense_ref, part_ref, sums_ref, mine_ref, sem,
):
    step = pl.program_id(0)

    @pl.when(step == 0)
    def _():
        first = pl.multiple_of(lax.axis_index("dom") * TILES, TILES)
        copy = pltpu.make_async_copy(atom_ref.at[pl.ds(first, TILES)], mine_ref, sem)
        copy.start()
        sums_ref[...] = jnp.zeros_like(sums_ref)
        hi, lo = split(x_ref[...])
        xhi_ref[...] = hi
        xlo_ref[...] = lo
        copy.wait()

    lo_ids = lax.broadcasted_iota(jnp.int32, (LO, TILE), 0).astype(F32).astype(BF16)
    pair_ids = (lax.broadcasted_iota(jnp.int32, (2 * NP, TILE), 0) // NP).astype(F32)
    one, zero = jnp.ones((), BF16), jnp.zeros((), BF16)

    def densify(group, carry):
        for i in range(GROUP):
            e = group * GROUP + i
            slot_ref[step * STEP_TILES + e] = slot_of(
                mine_ref[step * STEP_TILES + e], owner_ref
            )
            cells = cell_ref[pl.ds(e, 1), :]
            v_hi, v_lo = split(proj_ref[e])
            v_hi = jnp.concatenate([v_hi, v_hi], axis=0)
            v_lo = jnp.concatenate([v_lo, v_lo], axis=0)
            high = jnp.broadcast_to((cells // LO).astype(F32), (2 * NP, TILE)) - pair_ids
            high = high.astype(BF16)
            hits = [high == jnp.full((), 2.0 * h, BF16) for h in range(HI // 2)]
            spread = jnp.concatenate(
                [jnp.where(hit, v, zero) for v in (v_hi, v_lo) for hit in hits], axis=0
            )
            low = (cells & (LO - 1)).astype(F32).astype(BF16)
            hot = jnp.where(jnp.broadcast_to(low, (LO, TILE)) == lo_ids, one, zero)
            both = lax.dot_general(
                spread, hot, (((1,), (1,)), ((), ())), preferred_element_type=F32
            )
            sums = both[: HI * NP] + both[HI * NP :]
            rows = pl.ds(pl.multiple_of(e * NP, NP), NP)
            for h in range(HI):
                dense_ref[rows, h * LO : (h + 1) * LO] = sums[h * NP : (h + 1) * NP]
        return carry

    lax.fori_loop(0, STEP_TILES // GROUP, densify, 0)
    d_hi, d_lo = split(dense_ref[...])
    dhi_ref[...] = d_hi
    dlo_ref[...] = d_lo
    rows = STEP_TILES * NP
    dot = functools.partial(
        lax.dot_general, dimension_numbers=(((1,), (0,)), ((), ())), preferred_element_type=F32
    )
    upper = dot(jnp.concatenate([d_hi, d_lo], axis=0), xhi_ref[...])
    part_ref[...] = upper[:rows] + (upper[rows:] + dot(d_hi, xlo_ref[...]))

    def add(e, carry):
        slot = slot_ref[step * STEP_TILES + e]
        value = part_ref[pl.ds(pl.multiple_of(e * NP, NP), NP), :]
        sums_ref[slot] = sums_ref[slot] + value
        return carry

    lax.fori_loop(0, STEP_TILES, add, 0, unroll=8)

    @pl.when(step == TILES // STEP_TILES - 1)
    def _():
        keep_ref[...] = sums_ref[:SLOTS]
        send_ref[...] = sums_ref[SLOTS:ALL]


def project(tile_atom, atom_owner, projectors, tile_cells, x):
    rows = STEP_TILES * NP
    projectors, tile_cells, x = (in_hbm(v) for v in (projectors, tile_cells, x))
    return pl.pallas_call(
        project_kernel,
        out_shape=(
            jax.ShapeDtypeStruct((SLOTS, NP, W), F32),
            jax.ShapeDtypeStruct((SLOTS, NP, W), F32),
            pltpu.HBM((TILES * NP, CELLS), BF16),
            pltpu.HBM((TILES * NP, CELLS), BF16),
            jax.ShapeDtypeStruct((TILES,), jnp.int32),
        ),
        grid_spec=pltpu.PrefetchScalarGridSpec(
            num_scalar_prefetch=1,
            grid=(TILES // STEP_TILES,),
            in_specs=[
                pl.BlockSpec(memory_space=pl.ANY),
                pl.BlockSpec((STEP_TILES, NP, TILE), lambda i, *_: (i, 0, 0)),
                pl.BlockSpec((STEP_TILES, TILE), lambda i, *_: (i, 0)),
                pl.BlockSpec((CELLS, W), lambda i, *_: (0, 0)),
            ],
            out_specs=[
                pl.BlockSpec((SLOTS, NP, W), lambda i, *_: (0, 0, 0)),
                pl.BlockSpec((SLOTS, NP, W), lambda i, *_: (0, 0, 0)),
                pl.BlockSpec((rows, CELLS), lambda i, *_: (i, 0)),
                pl.BlockSpec((rows, CELLS), lambda i, *_: (i, 0)),
                pl.BlockSpec(memory_space=pltpu.SMEM),
            ],
            scratch_shapes=[
                pltpu.VMEM((CELLS, W), BF16),
                pltpu.VMEM((CELLS, W), BF16),
                pltpu.VMEM((rows, CELLS), F32),
                pltpu.VMEM((rows, W), F32),
                pltpu.VMEM((ALL + 1, NP, W), F32),
                pltpu.SMEM((TILES,), jnp.int32),
                pltpu.SemaphoreType.DMA(()),
            ],
        ),
        compiler_params=pltpu.CompilerParams(vmem_limit_bytes=VMEM),
        name="project",
    )(atom_owner, tile_atom, projectors, tile_cells, x)


def couple_kernel(coupling_ref, sums_ref, out_ref):
    sums = sums_ref[0]
    for z in range(1, Z):
        sums = sums + sums_ref[z]
    for r in range(OWN):
        matrix = coupling_ref[r]
        total = matrix[:, 0:1] * sums[r, 0:1, :]
        for j in range(1, NP):
            total = total + matrix[:, j : j + 1] * sums[r, j : j + 1, :]
        out_ref[r * NP : (r + 1) * NP, :] = total


def couple(coupling, sums):
    return pl.pallas_call(
        couple_kernel,
        out_shape=jax.ShapeDtypeStruct((OWN * NP, W), F32),
        compiler_params=SMALL,
        name="couple",
    )(coupling, sums)


def relative_rows(rotation_ref, offset):
    band = (lax.axis_index("band") + offset) & 3
    return rotation_ref[pl.ds(pl.multiple_of(band * W, W), W), :]


def turn_small_kernel(rhi_ref, rlo_ref, mine_ref, right_ref, far_ref, left_ref, out_ref):
    value = jnp.concatenate(
        [mine_ref[...], right_ref[...], far_ref[...], left_ref[...]], axis=1
    )
    total = dot3(*split(value), rhi_ref[...], rlo_ref[...], ((1,), (0,)))
    for z in range(Z):
        out_ref[z] = total


def turn_small(r_hi, r_lo, *pieces):
    return pl.pallas_call(
        turn_small_kernel,
        out_shape=jax.ShapeDtypeStruct((Z, OWN * NP, W), F32),
        compiler_params=SMALL,
        name="turn_small",
    )(r_hi, r_lo, *pieces)


ROWS = 512


def turn_rows(r_hi, r_lo, pieces, out_ref, xhi_ref, xlo_ref):
    for start in range(0, ROWS, W):
        part = slice(start, start + W)
        for offset, ref in enumerate(pieces):
            hi, lo = split(ref[part, :])
            xhi_ref[part, offset * W : (offset + 1) * W] = hi
            xlo_ref[part, offset * W : (offset + 1) * W] = lo
        out_ref[part, :] = dot3(
            xhi_ref[part, :], xlo_ref[part, :], r_hi[...], r_lo[...], ((1,), (0,))
        )


def turn_first_kernel(rotation_ref, *refs):
    pieces, (out_ref, rhi_ref, rlo_ref, xhi_ref, xlo_ref) = refs[:4], refs[4:]

    @pl.when(pl.program_id(0) == 0)
    def _():
        for offset in range(4):
            hi, lo = split(relative_rows(rotation_ref, offset))
            rhi_ref[offset * W : (offset + 1) * W, :] = hi
            rlo_ref[offset * W : (offset + 1) * W, :] = lo

    turn_rows(rhi_ref, rlo_ref, pieces, out_ref, xhi_ref, xlo_ref)


def turn_second_kernel(rhi_ref, rlo_ref, *refs):
    pieces, (out_ref, xhi_ref, xlo_ref) = refs[:4], refs[4:]
    turn_rows(rhi_ref, rlo_ref, pieces, out_ref, xhi_ref, xlo_ref)


TURN_STEPS = PLANE // ROWS
TURN_BLOCK = pl.BlockSpec((ROWS, W), lambda i: (i, 0))
TURN_WHOLE = pl.BlockSpec((4 * W, W), lambda i: (0, 0))
TURN_SCRATCH = [pltpu.VMEM((ROWS, 4 * W), BF16), pltpu.VMEM((ROWS, 4 * W), BF16)]


def turn_first(rotation, mine, right, far, left):
    return pl.pallas_call(
        turn_first_kernel,
        out_shape=(
            jax.ShapeDtypeStruct((PLANE, W), F32),
            jax.ShapeDtypeStruct((4 * W, W), BF16),
            jax.ShapeDtypeStruct((4 * W, W), BF16),
        ),
        grid_spec=pl.GridSpec(
            grid=(TURN_STEPS,),
            in_specs=[TURN_WHOLE] + [TURN_BLOCK] * 4,
            out_specs=[TURN_BLOCK, TURN_WHOLE, TURN_WHOLE],
            scratch_shapes=TURN_SCRATCH,
        ),
        compiler_params=MEDIUM,
        name="turn_first",
    )(rotation, mine, right, far, left)


def turn_second(r_hi, r_lo, mine, right, far, left):
    return pl.pallas_call(
        turn_second_kernel,
        out_shape=jax.ShapeDtypeStruct((PLANE, W), F32),
        grid_spec=pl.GridSpec(
            grid=(TURN_STEPS,),
            in_specs=[TURN_WHOLE] * 2 + [TURN_BLOCK] * 4,
            out_specs=TURN_BLOCK,
            scratch_shapes=TURN_SCRATCH,
        ),
        compiler_params=MEDIUM,
        name="turn_second",
    )(r_hi, r_lo, mine, right, far, left)


def stencil_kernel(level_ref, outer_ref, inner_ref, beyond_ref, out_ref, whole_ref):
    side = 32
    outer = outer_plane()

    def plane(index, mine_ref, other_ref, halo_ref):
        first = index * PLANE

        def line(y, carry):
            here = pl.ds(pl.multiple_of(y * side, side), side)
            above = pl.ds(pl.multiple_of(((y + side - 1) & (side - 1)) * side, side), side)
            below = pl.ds(pl.multiple_of(((y + 1) & (side - 1)) * side, side), side)
            there = pl.ds(pl.multiple_of(first + y * side, side), side)
            value = mine_ref[here, :]
            beside = other_ref[here, :]
            if halo_ref is not None:
                beside = beside + halo_ref[here, :]
            beside = beside + (mine_ref[above, :] + mine_ref[below, :])
            beside = beside + (pltpu.roll(value, 1, 0) + pltpu.roll(value, side - 1, 0))
            out_ref[there, :] = (3.0 + level_ref[there, :]) * value - 0.5 * beside
            whole_ref[there, :] = value
            return carry

        lax.fori_loop(0, side, line, 0, unroll=4)

    plane(outer, outer_ref, inner_ref, beyond_ref)
    plane(1 - outer, inner_ref, outer_ref, None)


def stencil(level, outer, inner, beyond):
    whole = pltpu.HBM((CELLS, W), F32)
    return pl.pallas_call(
        stencil_kernel,
        out_shape=(whole, whole),
        compiler_params=pltpu.CompilerParams(vmem_limit_bytes=24 << 20),
        name="stencil",
    )(level, in_hbm(outer), in_hbm(inner), beyond)


CUT = 1024
PIECES = (64, 32, 32, 32, 32, 32, 32)


def expand_kernel(*refs):
    count = C * len(PIECES)
    slot_ref, pieces = refs[0], refs[1 : 1 + count]
    dhi_ref, dlo_ref, local_ref, inside_ref = refs[1 + count : 5 + count]
    out_ref, all_ref, back_ref, bhi_ref, blo_ref = refs[5 + count :]
    step = pl.program_id(0)

    @pl.when(step == 0)
    def _():
        start = 0
        for i, piece in enumerate(pieces):
            size = PIECES[i % len(PIECES)]
            all_ref[start : start + size] = piece[...]
            start += size
        all_ref[ALL] = jnp.zeros((NP, W), F32)

        def take(e, carry):
            back_ref[pl.ds(pl.multiple_of(e * NP, NP), NP), :] = all_ref[slot_ref[e]]
            return carry

        lax.fori_loop(0, TILES, take, 0, unroll=16)
        hi, lo = split(back_ref[...].T)
        bhi_ref[...] = hi
        blo_ref[...] = lo

    plane = (step >= PLANE // CUT).astype(jnp.int32)
    weight = jnp.where(plane == outer_plane(), 0.0, 0.5)
    for start in range(0, CUT, W):
        part = slice(start, start + W)
        local = local_ref[part, :] - weight * inside_ref[part, :]
        far = dot3(bhi_ref[...], blo_ref[...], dhi_ref[:, part], dlo_ref[:, part], ((1,), (0,)))
        out_ref[part, :] = local + far.T


def expand(slots, pieces, d_hi, d_lo, local, inside):
    d_hi, d_lo, local = in_hbm(d_hi), in_hbm(d_lo), in_hbm(local)
    dense = pl.BlockSpec((TILES * NP, CUT), lambda i, *_: (0, i))
    return pl.pallas_call(
        expand_kernel,
        out_shape=jax.ShapeDtypeStruct((CELLS, W), F32),
        grid_spec=pltpu.PrefetchScalarGridSpec(
            num_scalar_prefetch=1,
            grid=(CELLS // CUT,),
            in_specs=[
                *[pl.BlockSpec(memory_space=pltpu.VMEM)] * len(pieces),
                dense,
                dense,
                pl.BlockSpec((CUT, W), lambda i, *_: (i, 0)),
                pl.BlockSpec((CUT, W), lambda i, *_: (i % (PLANE // CUT), 0)),
            ],
            out_specs=pl.BlockSpec((CUT, W), lambda i, *_: (i, 0)),
            scratch_shapes=[
                pltpu.VMEM((ALL + 1, NP, W), F32),
                pltpu.VMEM((TILES * NP, W), F32),
                pltpu.VMEM((W, TILES * NP), BF16),
                pltpu.VMEM((W, TILES * NP), BF16),
            ],
        ),
        compiler_params=pltpu.CompilerParams(vmem_limit_bytes=30 << 20),
        name="expand",
    )(slots, *pieces, d_hi, d_lo, local, inside)


def at(y, z, c):
    return (y % Y) * Z * C + (z % Z) * C + c


DEVICES = [(y, z, c) for y in range(Y) for z in range(Z) for c in range(C)]


def to_y(value, shift):
    return lax.ppermute(value, "dom", [(at(y, z, c), at(y + shift, z, c)) for y, z, c in DEVICES])


def to_core(value):
    return lax.ppermute(value, "dom", [(at(y, z, c), at(y, z, 1 - c)) for y, z, c in DEVICES])


def to_next_chip(value):
    count = Y * Z * C
    return lax.ppermute(
        value, "dom", [(i, (i + (1 if i % 2 else -1)) % count) for i in range(count)]
    )


def to_band(value, shift):
    return lax.ppermute(value, "band", [(i, (i + shift) % 4) for i in range(4)])


Z_LINES = [[at(y, z, c) for z in range(Z)] for y in range(Y) for c in range(C)]


def swap_z(value):
    return lax.all_to_all(
        value, "dom", split_axis=0, concat_axis=0, axis_index_groups=Z_LINES, tiled=True
    )


def step(orbitals, potential, projectors, tile_cells, tile_atom, atom_owner, coupling, rotation):
    x = orbitals.reshape(CELLS, W)

    outer, inner = cut_planes(x)
    left_a = to_band(outer, 1)
    right_b = to_band(inner, -1)
    right_a = to_band(outer, -1)
    far_a = to_band(left_a, 1)
    left_b = to_band(inner, 1)
    far_b = to_band(right_b, -1)

    keep, send, d_hi, d_lo, slots = project(
        tile_atom, atom_owner, projectors, tile_cells, x
    )
    send = to_core(send)
    sums = (keep + send).reshape(Y, Z, OWN, NP, W)
    cut = Z // 2
    up = to_y(sums[2, :cut], 1)
    down = to_y(sums[2, cut:], -1)
    up_raw = to_y(sums[1, cut:], 1)
    down_raw = to_y(sums[3, :cut], -1)
    up = to_y(sums[1, :cut] + up, 1)
    down = to_y(sums[3, cut:] + down, -1)
    line = sums[0] + jnp.concatenate([up + down_raw, up_raw + down], axis=0)
    line = swap_z(line)
    scaled = couple(coupling, line)

    outer, r_hi, r_lo = turn_first(rotation, outer, right_a, far_a, left_a)
    beyond = to_next_chip(outer)
    inner = turn_second(r_hi, r_lo, inner, right_b, far_b, left_b)
    inside = to_core(inner)
    level = potential.reshape(CELLS, 1)
    local, turned = stencil(level, outer, inner, beyond)

    parts = to_band(scaled, -1), to_band(scaled, 2), to_band(scaled, 1)
    back = turn_small(r_hi, r_lo, scaled, *parts)

    line = swap_z(back).reshape(Z * OWN, NP, W)
    mid = Z * OWN // 2
    below_low = to_y(line[:mid], 1)
    above_high = to_y(line[mid:], -1)
    below_high = to_y(line[mid:], 1)
    above_low = to_y(line[:mid], -1)
    across_a = to_y(below_low, 1)
    across_b = to_y(above_high, -1)
    near = [line, above_low, above_high, across_a, across_b, below_low, below_high]
    pieces = near + [to_core(v) for v in near]
    applied = expand(slots, pieces, d_hi, d_lo, local, inside)
    return turned.reshape(orbitals.shape), applied.reshape(orbitals.shape)


def solution(mesh):
    return jax.shard_map(
        step,
        mesh=mesh,
        in_specs=(
            P("dom", None, None, "band"),
            P("dom", None, None),
            P("dom", None, None),
            P("dom", None),
            P(),
            P(),
            P("dom", None, None),
            P(None, "band"),
        ),
        out_specs=(P("dom", None, None, "band"), P("dom", None, None, "band")),
        check_vma=False,
    )
```
